32 devices in a mesh: dp: 16 (over z, x, core), sub: 2 (over y).
Axes of the slice: x: 2, y: 2, z: 4, core: 2. Of those that a mesh axis runs over, the one named last changes fastest.
Arguments:
- context: bfloat16 [50432, 1024], P(('dp', 'sub')), may hold values from -6 to 6
- target: bfloat16 [50432, 1024], P(('dp', 'sub')), may hold values from -16 to 16
- weight: float32 [1024, 1024], P(('dp', 'sub')), may hold values from -0.1875 to 0.1875
- stale: bfloat16 [32, 1024, 1024], P(('dp', 'sub')), may hold values from -0.3984375 to 0.3984375
- trigger: int32 [32, 16], P(('dp', 'sub')), may hold values 0 or 1
- aggregate: float32 [1024, 1024], P(('dp', 'sub')), may hold values from -3 to 3
- moment: float32 [1024, 1024], P(('dp', 'sub')), may hold values from -0.6 to 0.6
- second: float32 [1024, 1024], P(('dp', 'sub')), may hold values from 0.0001 to 0.01
Outputs:
- aggregate_new: float32 [1024, 1024], P(('dp', 'sub'))
- weight_new: float32 [1024, 1024], P(('dp', 'sub'))
- moment_new: float32 [1024, 1024], P(('dp', 'sub'))
- second_new: float32 [1024, 1024], P(('dp', 'sub'))
- stale_new: bfloat16 [32, 1024, 1024], P(('dp', 'sub'))
- norms: float32 [16], replicated
The draws below stay inside these ranges and needn't reach their ends.
All inputs are finite; a program needn't handle non-finite values. No bound on the sum of `trigger` on one device may be relied on, other than what follows from the above.
Results may differ from the reference program's by a relative error of at most 0.006.
Values may be sent and summed in bfloat16 or wider, within the bound.
No kernel may reach another device: no remote copies, remote signals or barrier semaphores. Data moves between devices by JAX's collectives and lax.ppermute only.
A program may use at most 64 MiB of HBM per device.

```python
import math
import jax
import jax.numpy as jnp
from jax import lax

D = 1024
BLOCKS = 16
ROWS = 1576
TOKENS = 50432
N_DP = 16
N_SUB = 2


def draw_target(key, part):
    rows = jnp.arange(TOKENS, dtype=jnp.float32)
    rising = 1.0 + 2.0 * rows / TOKENS
    base = jax.random.truncated_normal(key, -4.0, 4.0, (TOKENS, D), jnp.float32)
    values = base * rising[:, None]
    return values.astype(jnp.bfloat16)


def touch_ends(entries, stream_key, low, high):
    dims = entries.shape
    index_at = [jax.random.randint(jax.random.fold_in(stream_key, axis), (), 0, dims[axis]) for axis in range(len(dims))]
    entries = entries.at[tuple(index_at)].set(low)
    longest = dims.index(max(dims))
    index_at[longest] = (index_at[longest] + 1) % dims[longest]
    return entries.at[tuple(index_at)].set(high)


def raised(entries, own_key, source, target, parts, factor):
    owner, partner = [(jnp.arange(entries.shape[position]) // (entries.shape[position] // parts)).reshape([-1 if axis == position else 1 for axis in range(entries.ndim)]) for position in (source, target)]
    chosen = jax.random.permutation(own_key, parts)[partner]
    strong = (owner == chosen) | (owner == (partner + parts // 2) % parts)
    return jnp.where(strong, factor * entries, entries)


def shard_levels(stream_key, dims, shards, smallest, high):
    level, own = 1.0, jax.random.fold_in(stream_key, 6)
    for position, parts in shards:
        steps = jnp.exp(jax.random.uniform(jax.random.fold_in(own, position), (parts,), jnp.float32, smallest / len(shards), high / len(shards)))
        level = level * jnp.repeat(steps, dims[position] // parts).reshape([-1 if axis == position else 1 for axis in range(len(dims))])
    return level


def gaussian(own_key, dims, spread, most, cuts=(), kind=jnp.bfloat16):
    values = jax.random.normal(own_key, dims, jnp.float32) * spread
    if len(cuts) > 0:
        values = shard_levels(own_key, dims, cuts, -0.22, 0.18) * values
    return jnp.clip(values, min=-most, max=most).astype(kind)


def noise_with(key, shape, width, reach, shards, heavy, kind=jnp.bfloat16):
    drawn = width * jax.random.normal(key, shape, jnp.float32)
    if shards:
        drawn = drawn * shard_levels(key, shape, shards, -0.22, 0.18)
    return jnp.clip(raised(drawn, jax.random.fold_in(key, 3), *heavy), -reach, reach).astype(kind)


def setup_inputs(seed: int = 0) -> dict:
    splits = jax.random.split(jax.random.key(seed), 9)
    return {
        "context": gaussian(splits[0], (TOKENS, D), 1.0, 6.0, ((0, 32),)),
        "target": draw_target(jax.random.fold_in(splits[8], 71), 0),
        "weight": gaussian(splits[2], (D, D), D ** -0.5, 0.1875, ((0, 32),), jnp.float32),
        "stale": noise_with(splits[3], (N_DP * N_SUB, D, D), 0.05, 0.3984375, ((0, 32),), (0, 1, 32, 2.75)),
        "trigger": touch_ends((jax.random.randint(splits[4], (N_DP * N_SUB, BLOCKS), 0, 2) < 1).astype(jnp.int32), jax.random.fold_in(splits[4], 1), 0, 1),
        "aggregate": gaussian(splits[5], (D, D), 0.5, 3.0, ((0, 32),), jnp.float32),
        "moment": gaussian(splits[6], (D, D), 0.1, 0.6, ((0, 32),), jnp.float32),
        "second": jnp.clip(jnp.exp(math.log(0.01) - 4.6051702 * jax.random.uniform(splits[7], (D, D), jnp.float32) ** shard_levels(splits[7], (D, D), ((0, 32),), -0.2, 0.2)), 0.0001, 0.01),
    }


def reference(context, target, weight, stale, trigger, aggregate, moment, second):
    devices = N_DP * N_SUB
    low = weight.astype(jnp.bfloat16)
    span = D // BLOCKS

    def one(carry, index):
        total, squares = carry
        rows_ctx = lax.dynamic_slice_in_dim(context, index * ROWS, ROWS, 0)
        rows_tgt = lax.dynamic_slice_in_dim(target, index * ROWS, ROWS, 0)
        output = jnp.dot(rows_ctx, low, preferred_element_type=jnp.float32)
        error = (output - rows_tgt.astype(jnp.float32)).astype(jnp.bfloat16)
        grad = lax.dot_general(rows_ctx, error, (((0,), (0,)), ((), ())), preferred_element_type=jnp.float32) / ROWS
        old = lax.dynamic_index_in_dim(stale, index, 0, keepdims=False).astype(jnp.float32)
        flags = lax.dynamic_index_in_dim(trigger, index, 0, keepdims=False).astype(jnp.float32)
        diff = grad - old
        blocked = diff.reshape(BLOCKS, span, D)
        squares = squares + lax.optimization_barrier(jnp.sum(blocked * blocked, axis=(1, 2)))
        chosen = (blocked * flags[:, None, None]).reshape(D, D)
        fresh = (flags[:, None, None] * grad.reshape(BLOCKS, span, D) + (1.0 - flags[:, None, None]) * old.reshape(BLOCKS, span, D)).reshape(D, D)
        return ((total + chosen, squares), fresh.astype(jnp.bfloat16))
    start = (jnp.zeros((D, D), jnp.float32), jnp.zeros((BLOCKS,), jnp.float32))
    (total, norms), stale_new = lax.scan(one, start, jnp.arange(devices, dtype=jnp.int32))
    aggregate_new = aggregate + total
    moment_new = 0.9 * moment + 0.1 * aggregate_new
    second_new = 0.999 * second + 0.001 * aggregate_new * aggregate_new
    weight_new = weight - 0.001 * (moment_new / (jnp.sqrt(second_new) + 1e-08) + 0.05 * weight)
    return (aggregate_new, weight_new, moment_new, second_new, stale_new, norms)
```

```python
import functools
import itertools

import jax
import jax.numpy as jnp
from jax import lax
from jax.experimental import pallas as pl
from jax.experimental.pallas import tpu as pltpu
from jax.sharding import PartitionSpec as P

AXES = ("dp", "sub")
LANES = 128
EXTRA = 8


class Grid:
    def __init__(self, n_dp, n_sub):
        cores = 2 if n_dp % 2 == 0 else 1
        rest = n_dp // cores
        outer = max(d for d in range(1, rest + 1) if rest % d == 0 and d * d <= 2 * rest)
        self.sizes = (outer, rest // outer, cores, n_sub)

    def index(self, digits):
        i = 0
        for d, n in zip(digits, self.sizes):
            i = i * n + d % n
        return i

    def perm(self, shift):
        pairs = []
        for at in itertools.product(*map(range, self.sizes)):
            pairs.append((self.index(at), self.index([a + s for a, s in zip(at, shift)])))
        return pairs

    def near(self):
        return [(0, dx, 0, dy) for dx in range(self.sizes[1]) for dy in range(self.sizes[3])]

    def along(self):
        return [(dz, 0, 0, 0) for dz in range(self.sizes[0])]

    def cores(self):
        return [(0, 0, dc, 0) for dc in range(self.sizes[2])]


def block_at(grid, pos, shift, sign):
    i = 0
    for p, s, n in zip(pos, shift, grid.sizes):
        d = p if s == 0 else lax.rem(p + (sign * s) % n, n)
        i = i * n + d
    return i


def plus(*shifts):
    return tuple(sum(s) for s in zip(*shifts))


def norm_rows(total):
    row = lax.broadcasted_iota(jnp.int32, total.shape, 0)
    high = total.astype(jnp.bfloat16).astype(jnp.float32)
    rest = total - high
    mid = rest.astype(jnp.bfloat16).astype(jnp.float32)
    low = rest - mid
    out = jnp.where(row == 0, high, jnp.where(row == 1, mid, jnp.where(row == 2, low, 0.0)))
    return out.astype(jnp.bfloat16)


def read_norms(rows):
    total = jnp.sum(rows.astype(jnp.float32), axis=0, keepdims=True)
    return jnp.broadcast_to(total, rows.shape)


def main_kernel(grid, owned, blocks, rows, pos_ref, trig_ref, *refs):
    outer, inner, cores, n_sub = grid.sizes
    near = grid.near()
    n_pieces = cores * len(near)
    pieces, refs = refs[:n_pieces], refs[n_pieces:]
    ghi_ref, glo_ref, b_ref, old_ref, new_ref, send_ref, own_ref, w_ref = refs
    width = ghi_ref.shape[0]
    span = width // blocks
    pos = [pos_ref[k] for k in range(4)]
    for k, (dc, dn) in enumerate(itertools.product(grid.cores(), near)):
        for dz in grid.along():
            at = pl.multiple_of(block_at(grid, pos, plus(dc, dn, dz), -1) * owned, owned)
            w_ref[pl.ds(at, owned), :] = pieces[k][pl.ds(dz[0] * owned, owned), :]
    lane = lax.broadcasted_iota(jnp.int32, (EXTRA, width), 1)
    norms = jnp.zeros((EXTRA, width), jnp.float32)
    per_core = blocks // cores
    group = min(4, per_core)
    w = w_ref[...]
    for half in range(cores):
        core = lax.rem(pos[2] + 1 + half, cores)
        for g in range(per_core // group):
            ids = [(g * group + k) * cores + core for k in range(group)]
            starts = [pl.multiple_of(b * span, span) for b in ids]
            hi = jnp.concatenate([ghi_ref[pl.ds(s, span), :] for s in starts], axis=0)
            lo = jnp.concatenate([glo_ref[pl.ds(s, span), :] for s in starts], axis=0)
            acc = jnp.dot(hi, w, preferred_element_type=jnp.float32)
            acc = acc + jnp.dot(lo, w, preferred_element_type=jnp.float32)
            for k in range(group):
                b, s = ids[k], starts[k]
                grad = (acc[k * span : (k + 1) * span] - b_ref[pl.ds(s, span), :]) / rows
                old = old_ref[pl.ds(s, span), :].astype(jnp.float32)
                flag = trig_ref[b].astype(jnp.float32)
                diff = grad - old
                square = jnp.sum(diff * diff)
                norms = jnp.where(lane == b, square, norms)
                new_ref[pl.ds(s, span), :] = (flag * grad + (1.0 - flag) * old).astype(jnp.bfloat16)
                chosen = diff * flag
                zx = g * group + k
                z, x = zx // inner, zx % inner
                dz = lax.rem(z - pos[0] + outer, outer)
                dx = lax.rem(x - pos[1] + inner, inner)
                for y in range(n_sub):
                    dy = lax.rem(y - pos[3] + n_sub, n_sub)
                    at = pl.multiple_of((((dx * n_sub + dy) * outer) + dz) * owned, owned)
                    part = chosen[y * owned : (y + 1) * owned]
                    if half == cores - 1:
                        own_ref[pl.ds(at, owned), :] = part
                    else:
                        send_ref[pl.ds(at, owned), :] = part.astype(jnp.bfloat16)
    per = per_core * span
    send_ref[per:, :] = norm_rows(norms)
    own_ref[per:, :] = norms


def main_plain(grid, owned, blocks, rows, pos, trigger, *arrays):
    near = grid.near()
    *pieces, g_high, g_low, cross, old = arrays
    width = g_high.shape[0]
    span = width // blocks
    shifts = [
        plus(dc, dn, dz) for dc, dn, dz in itertools.product(grid.cores(), near, grid.along())
    ]
    place = jnp.stack([jnp.asarray(block_at(grid, pos, s, -1)) for s in shifts])
    stack = jnp.concatenate(pieces, axis=0).reshape(len(shifts), owned, width)
    w = jnp.zeros_like(stack).at[place].set(stack, unique_indices=True).reshape(width, width)
    acc = jnp.dot(g_high, w, preferred_element_type=jnp.float32)
    acc = acc + jnp.dot(g_low, w, preferred_element_type=jnp.float32)
    grad = (acc - cross) / rows
    old = old.astype(jnp.float32)
    flags = jnp.repeat(trigger.astype(jnp.float32), span)[:, None]
    diff = grad - old
    stale_new = (flags * grad + (1.0 - flags) * old).astype(jnp.bfloat16)
    squares = jnp.sum((diff * diff).reshape(blocks, span * width), axis=1)
    norms = jnp.broadcast_to(jnp.pad(squares, (0, width - blocks)), (EXTRA, width))
    chosen = (diff * flags).reshape(len(shifts), owned, width)
    ends = []
    for dc in (*grid.cores()[1:], grid.cores()[0]):
        to = jnp.stack(
            [jnp.asarray(block_at(grid, pos, plus(dc, dn, dz), 1)) for dn, dz in itertools.product(near, grid.along())]
        )
        ends.append(chosen[to].reshape(-1, width))
    send = jnp.concatenate([ends[0].astype(jnp.bfloat16), norm_rows(norms)], axis=0)
    return stale_new, send, jnp.concatenate([ends[1], norms], axis=0)


def near_kernel(n_near, own_ref, got_ref, keep_ref, *send_refs):
    total = own_ref.shape[0] - EXTRA
    size = total // n_near
    norms = own_ref[total:, :] + read_norms(got_ref[total:, :])
    keep_ref[:size, :] = own_ref[:size, :] + got_ref[:size, :].astype(jnp.float32)
    keep_ref[size:, :] = norms
    coded = norm_rows(norms)
    for k, ref in enumerate(send_refs, 1):
        part = slice(k * size, (k + 1) * size)
        ref[:size, :] = (own_ref[part, :] + got_ref[part, :].astype(jnp.float32)).astype(jnp.bfloat16)
        ref[size:, :] = coded


def along_kernel(outer, n_near, keep_ref, *refs):
    got, outs = refs[: n_near - 1], refs[n_near - 1 :]
    size = keep_ref.shape[0] - EXTRA
    owned = size // outer
    total = keep_ref[:size, :]
    norms = keep_ref[size:, :]
    for ref in got:
        total = total + ref[:size, :].astype(jnp.float32)
        norms = norms + read_norms(ref[size:, :])
    outs[0][:owned, :] = total[:owned]
    outs[0][owned:, :] = norms
    coded = norm_rows(norms)
    for k, ref in enumerate(outs[1:], 1):
        ref[:owned, :] = total[k * owned : (k + 1) * owned].astype(jnp.bfloat16)
        ref[owned:, :] = coded


def final_kernel(keep_ref, *refs):
    got, refs = refs[:-8], refs[-8:]
    agg_ref, weight_ref, moment_ref, second_ref, agg_out, weight_out, moment_out, second_out = refs[:8]
    owned = agg_ref.shape[0]
    total = keep_ref[:owned, :]
    for ref in got:
        total = total + ref[:owned, :].astype(jnp.float32)
    agg = agg_ref[...] + total
    moment = 0.9 * moment_ref[...] + 0.1 * agg
    second = 0.999 * second_ref[...] + 0.001 * agg * agg
    weight = weight_ref[...]
    agg_out[...] = agg
    moment_out[...] = moment
    second_out[...] = second
    weight_out[...] = weight - 0.001 * (moment / (jnp.sqrt(second) + 1e-08) + 0.05 * weight)


def call(kernel, shapes, n_in, scratch=(), scalars=0):
    vmem = pl.BlockSpec(memory_space=pltpu.VMEM)
    smem = pl.BlockSpec(memory_space=pltpu.SMEM)
    return pl.pallas_call(
        kernel,
        out_shape=shapes,
        in_specs=[smem] * scalars + [vmem] * n_in,
        out_specs=[vmem] * len(shapes),
        scratch_shapes=list(scratch),
        compiler_params=pltpu.CompilerParams(vmem_limit_bytes=56 * 1024 * 1024),
    )


def body(grid, context, target, weight, stale, trigger, aggregate, moment, second):
    rows = context.shape[0]
    width = context.shape[1]
    owned = weight.shape[0]
    blocks = trigger.shape[1]
    outer, inner, cores, n_sub = grid.sizes
    near, along = grid.near(), grid.along()
    me = lax.axis_index("dp") * n_sub + lax.axis_index("sub")
    pos = jnp.stack(
        [me // (inner * cores * n_sub), me // (cores * n_sub) % inner, me // n_sub % cores, me % n_sub]
    ).astype(jnp.int32)

    def move(value, shift):
        return lax.ppermute(value, AXES, grid.perm(shift))

    low = weight.astype(jnp.bfloat16)
    line = jnp.concatenate([low] + [move(low, d) for d in along[1:]], axis=0)
    mine = [line] + [move(line, d) for d in near[1:]]
    pieces = list(mine)
    for dc in grid.cores()[1:]:
        pieces += [move(p, dc) for p in mine]

    over_tokens = (((0,), (0,)), ((), ()))
    square = lax.dot_general(context, context, over_tokens, preferred_element_type=jnp.float32)
    high = lax.reduce_precision(square, 8, 7)
    g_high = high.astype(jnp.bfloat16)
    g_low = (square - high).astype(jnp.bfloat16)
    cross = lax.dot_general(context, target, over_tokens, preferred_element_type=jnp.float32)

    f32, bf16 = jnp.float32, jnp.bfloat16
    part = width // cores
    shape = jax.ShapeDtypeStruct
    main = functools.partial(main_plain, grid, owned, blocks, rows)
    if blocks == outer * inner * cores and owned % (2 * EXTRA) == 0:
        main = call(
            functools.partial(main_kernel, grid, owned, blocks, rows),
            [shape((width, width), bf16), shape((part + EXTRA, width), bf16), shape((part + EXTRA, width), f32)],
            len(pieces) + 4,
            [pltpu.VMEM((width, width), bf16)],
            scalars=2,
        )
    stale_new, send, own = main(pos, trigger[0], *pieces, g_high, g_low, cross, stale[0])
    got = move(send, grid.cores()[1])
    size = part // len(near)
    keep, *sends = call(
        functools.partial(near_kernel, len(near)),
        [shape((size + EXTRA, width), f32)] + [shape((size + EXTRA, width), bf16)] * (len(near) - 1),
        2,
    )(own, got)
    got = [move(s, d) for s, d in zip(sends, near[1:])]
    keep, *sends = call(
        functools.partial(along_kernel, outer, len(near)),
        [shape((owned + EXTRA, width), f32)] + [shape((owned + EXTRA, width), bf16)] * (outer - 1),
        len(near),
    )(keep, *got)
    got = [move(s, d) for s, d in zip(sends, along[1:])]
    aggregate_new, weight_new, moment_new, second_new = call(
        final_kernel, [shape((owned, width), f32)] * 4, 1 + len(got) + 4
    )(keep, *got, aggregate, weight, moment, second)
    norms = keep[owned, :blocks]
    for g in got:
        norms = norms + jnp.sum(g[owned:, :blocks].astype(f32), axis=0)
    return (aggregate_new, weight_new, moment_new, second_new, stale_new[None], norms)


def solution(mesh):
    grid = Grid(mesh.shape["dp"], mesh.shape["sub"])
    split = P(("dp", "sub"), None)
    deep = P(("dp", "sub"), None, None)
    return jax.shard_map(
        functools.partial(body, grid),
        mesh=mesh,
        in_specs=(split, split, split, deep, split, split, split, split),
        out_specs=(split, split, split, split, deep, P()),
        check_vma=False,
    )
```

```python
import functools
import itertools

import jax
import jax.numpy as jnp
from jax import lax
from jax.experimental import pallas as pl
from jax.experimental.pallas import tpu as pltpu
from jax.sharding import PartitionSpec as P

AXES = ("dp", "sub")
LANES = 128
EXTRA = 8


class Grid:
    def __init__(self, n_dp, n_sub):
        cores = 2 if n_dp % 2 == 0 else 1
        rest = n_dp // cores
        outer = max(d for d in range(1, rest + 1) if rest % d == 0 and d * d <= 2 * rest)
        self.sizes = (outer, rest // outer, cores, n_sub)

    def index(self, digits):
        i = 0
        for d, n in zip(digits, self.sizes):
            i = i * n + d % n
        return i

    def perm(self, shift):
        pairs = []
        for at in itertools.product(*map(range, self.sizes)):
            pairs.append((self.index(at), self.index([a + s for a, s in zip(at, shift)])))
        return pairs

    def near(self):
        return [(0, dx, 0, dy) for dx in range(self.sizes[1]) for dy in range(self.sizes[3])]

    def along(self):
        return [(dz, 0, 0, 0) for dz in range(self.sizes[0])]

    def cores(self):
        return [(0, 0, dc, 0) for dc in range(self.sizes[2])]


def block_at(grid, pos, shift, sign):
    i = 0
    for p, s, n in zip(pos, shift, grid.sizes):
        d = p if s == 0 else lax.rem(p + (sign * s) % n, n)
        i = i * n + d
    return i


def position(grid):
    outer, inner, cores, n_sub = grid.sizes
    at = lax.axis_index("dp")
    digits = (lax.div(at, inner * cores), lax.rem(lax.div(at, cores), inner), lax.rem(at, cores))
    return [d.astype(jnp.int32) for d in (*digits, lax.axis_index("sub"))]


def plus(*shifts):
    return tuple(sum(s) for s in zip(*shifts))


def coded(total):
    row = lax.broadcasted_iota(jnp.int32, total.shape, 0)
    high = total.astype(jnp.bfloat16).astype(jnp.float32)
    rest = total - high
    mid = rest.astype(jnp.bfloat16).astype(jnp.float32)
    low = rest - mid
    out = jnp.where(row == 0, high, jnp.where(row == 1, mid, jnp.where(row == 2, low, 0.0)))
    return out.astype(jnp.bfloat16)


def decoded(rows):
    total = jnp.sum(rows.astype(jnp.float32), axis=0, keepdims=True)
    return jnp.broadcast_to(total, rows.shape)


def product(grid, owned, blocks, rows, core, trig_ref, ghi_ref, glo_ref, b_ref, old_ref, w, put_new, put_chosen):
    outer, inner, cores, n_sub = grid.sizes
    pos = position(grid)
    width = ghi_ref.shape[0]
    span = width // blocks
    lane = lax.broadcasted_iota(jnp.int32, (EXTRA, lanes_of(blocks)), 1)
    norms = jnp.zeros((EXTRA, lanes_of(blocks)), jnp.float32)
    per_core = blocks // cores
    group = min(4, per_core)
    for g in range(per_core // group):
        ids = [(g * group + k) * cores + core for k in range(group)]
        starts = [pl.multiple_of(b * span, span) for b in ids]
        hi = jnp.concatenate([ghi_ref[pl.ds(s, span), :] for s in starts], axis=0)
        lo = jnp.concatenate([glo_ref[pl.ds(s, span), :] for s in starts], axis=0)
        acc = jnp.dot(hi, w, preferred_element_type=jnp.float32)
        acc = acc + jnp.dot(lo, w, preferred_element_type=jnp.float32)
        for k in range(group):
            b, s = ids[k], starts[k]
            grad = (acc[k * span : (k + 1) * span] - b_ref[pl.ds(s, span), :]) / rows
            old = old_ref[pl.ds(s, span), :].astype(jnp.float32)
            flag = trig_ref[b].astype(jnp.float32)
            diff = grad - old
            norms = jnp.where(lane == b, jnp.sum(diff * diff), norms)
            zx = g * group + k
            put_new(zx, s, (flag * grad + (1.0 - flag) * old).astype(jnp.bfloat16))
            chosen = diff * flag
            z, x = zx // inner, zx % inner
            dz = lax.rem(z - pos[0] + outer, outer)
            dx = lax.rem(x - pos[1] + inner, inner)
            for y in range(n_sub):
                dy = lax.rem(y - pos[3] + n_sub, n_sub)
                at = pl.multiple_of((((dx * n_sub + dy) * outer) + dz) * owned, owned)
                put_chosen(at, chosen[y * owned : (y + 1) * owned])
    return norms


def send_kernel(grid, owned, blocks, rows, trig_ref, *refs):
    outer, inner, cores, n_sub = grid.sizes
    near = grid.near()
    pieces, refs = refs[: 2 * cores * len(near)], refs[2 * cores * len(near) :]
    ghi_ref, glo_ref, b_ref, old_ref, w_ref, new_ref, send_ref, norm_ref = refs
    pos = position(grid)
    span = ghi_ref.shape[0] // blocks
    for k, (dc, dn) in enumerate(itertools.product(grid.cores(), near)):
        for dz in grid.along():
            at = pl.multiple_of(block_at(grid, pos, plus(dc, dn, dz), -1) * owned, owned)
            piece = pieces[2 * k + (dz[0] > 0)]
            skip = max(dz[0] - 1, 0) * owned
            w_ref[pl.ds(at, owned), :] = piece[pl.ds(skip, owned), :]

    def put_new(i, start, value):
        new_ref[pl.ds(i * span, span), :] = value

    def put_chosen(at, value):
        send_ref[pl.ds(at, owned), :] = value.astype(jnp.bfloat16)

    core = lax.rem(pos[2] + 1, cores)
    norm_ref[...] = product(
        grid, owned, blocks, rows, core, trig_ref, ghi_ref, glo_ref, b_ref, old_ref, w_ref[...], put_new, put_chosen
    )


def keep_kernel(grid, owned, blocks, rows, trig_ref, w_ref, ghi_ref, glo_ref, b_ref, old_ref, half_ref, before_ref, *outs):
    new_ref, own_ref, norm_ref = outs
    cores = grid.sizes[2]
    pos = position(grid)
    span = ghi_ref.shape[0] // blocks

    def put_new(i, start, value):
        new_ref[pl.ds(start, span), :] = value

    def put_chosen(at, value):
        own_ref[pl.ds(at, owned), :] = value

    other = lax.rem(pos[2] + 1, cores)
    for i in range(blocks // cores):
        at = pl.multiple_of((i * cores + other) * span, span)
        new_ref[pl.ds(at, span), :] = half_ref[pl.ds(i * span, span), :]
    norm_ref[...] = before_ref[...] + product(
        grid, owned, blocks, rows, pos[2], trig_ref, ghi_ref, glo_ref, b_ref, old_ref, w_ref[...], put_new, put_chosen
    )


def main_kernels(grid, owned, blocks, rows, trigger, pieces, g_high, g_low, cross, old):
    f32, bf16 = jnp.float32, jnp.bfloat16
    width = g_high.shape[0]
    part = width // grid.sizes[2]
    shape = jax.ShapeDtypeStruct
    norm = shape((EXTRA, lanes_of(blocks)), f32)
    w, half, send, norms = call(
        functools.partial(send_kernel, grid, owned, blocks, rows),
        [shape((width, width), bf16), shape((part, width), bf16), shape((part, width), bf16), norm],
        len(pieces) + 4,
        scalars=1,
        limit=28,
    )(trigger, *pieces, g_high, g_low, cross, old)
    stale_new, own, norms = call(
        functools.partial(keep_kernel, grid, owned, blocks, rows),
        [shape((width, width), bf16), shape((part, width), f32), norm],
        7,
        scalars=1,
        limit=28,
    )(trigger, w, g_high, g_low, cross, old, half, norms)
    return stale_new, send, own, norms


def main_plain(grid, owned, blocks, rows, trigger, pieces, g_high, g_low, cross, old):
    near, along = grid.near(), grid.along()
    pos = position(grid)
    width = g_high.shape[0]
    span = width // blocks
    shifts = []
    for dc, dn in itertools.product(grid.cores(), near):
        shifts += [plus(dc, dn, dz) for dz in along]
    place = jnp.stack([jnp.asarray(block_at(grid, pos, s, -1)) for s in shifts])
    stack = jnp.concatenate(pieces, axis=0).reshape(len(shifts), owned, width)
    w = jnp.zeros_like(stack).at[place].set(stack, unique_indices=True).reshape(width, width)
    acc = jnp.dot(g_high, w, preferred_element_type=jnp.float32)
    acc = acc + jnp.dot(g_low, w, preferred_element_type=jnp.float32)
    grad = (acc - cross) / rows
    old = old.astype(jnp.float32)
    flags = jnp.repeat(trigger.astype(jnp.float32), span)[:, None]
    diff = grad - old
    stale_new = (flags * grad + (1.0 - flags) * old).astype(jnp.bfloat16)
    squares = jnp.sum((diff * diff).reshape(blocks, span * width), axis=1)
    norms = jnp.broadcast_to(jnp.pad(squares, (0, lanes_of(blocks) - blocks)), (EXTRA, lanes_of(blocks)))
    chosen = (diff * flags).reshape(len(shifts), owned, width)
    ends = []
    for dc in (*grid.cores()[1:], grid.cores()[0]):
        to = jnp.stack(
            [jnp.asarray(block_at(grid, pos, plus(dc, dn, dz), 1)) for dn, dz in itertools.product(near, along)]
        )
        ends.append(chosen[to].reshape(-1, width))
    return stale_new, ends[0].astype(jnp.bfloat16), ends[1], norms


def near_kernel(n_near, owned, own_ref, got_ref, keep_ref, rest_ref, *send_refs):
    size = own_ref.shape[0] // n_near
    keep_ref[...] = own_ref[:size, :] + got_ref[:size, :].astype(jnp.float32)
    for k, ref in enumerate(send_refs, 1):
        part = slice(k * size, (k + 1) * size)
        total = (own_ref[part, :] + got_ref[part, :].astype(jnp.float32)).astype(jnp.bfloat16)
        rest_ref[(k - 1) * owned : k * owned, :] = total[:owned]
        ref[...] = total[owned:]


def along_kernel(n_along, n_near, keep_ref, rest_ref, norm_ref, *refs):
    norm_refs, got, outs = refs[: n_along - 1], refs[n_along - 1 : n_along + n_near - 2], refs[n_along + n_near - 2 :]
    own_ref, total_ref, outs = outs[0], outs[1], outs[2:]
    owned = keep_ref.shape[0] // n_along
    norms = norm_ref[...]
    for ref in norm_refs:
        norms = norms + ref[...]
    total_ref[...] = norms
    total = keep_ref[owned:, :]
    for ref in got:
        total = total + ref[...].astype(jnp.float32)
    own_ref[...] = keep_ref[:owned, :]
    for k in range(n_along - 1):
        outs[k][...] = total[k * owned : (k + 1) * owned].astype(jnp.bfloat16)
    lanes = norms.shape[1]
    for k in range(n_near - 1):
        ref = outs[n_along - 1 + k]
        ref[:owned, :] = rest_ref[k * owned : (k + 1) * owned, :]
        ref[owned:, :] = jnp.zeros((EXTRA, keep_ref.shape[1]), jnp.bfloat16)
        ref[owned:, :lanes] = coded(norms)


def final_kernel(n_along, n_near, own_ref, norm_ref, *refs):
    along, near, refs = refs[: n_along - 1], refs[n_along - 1 : n_along + n_near - 2], refs[n_along + n_near - 2 :]
    agg_ref, weight_ref, moment_ref, second_ref, agg_out, weight_out, moment_out, second_out, norm_out = refs
    owned = agg_ref.shape[0]
    lanes = norm_ref.shape[1]
    total = own_ref[...]
    norms = norm_ref[...]
    for ref in along:
        total = total + ref[...].astype(jnp.float32)
    for ref in near:
        total = total + ref[:owned, :].astype(jnp.float32)
        norms = norms + decoded(ref[owned:, :lanes])
    agg = agg_ref[...] + total
    moment = 0.9 * moment_ref[...] + 0.1 * agg
    second = 0.999 * second_ref[...] + 0.001 * agg * agg
    weight = weight_ref[...]
    agg_out[...] = agg
    moment_out[...] = moment
    second_out[...] = second
    weight_out[...] = weight - 0.001 * (moment / (jnp.sqrt(second) + 1e-08) + 0.05 * weight)
    norm_out[...] = norms


def lanes_of(blocks):
    return -(-blocks // LANES) * LANES


def call(kernel, shapes, n_in, scalars=0, limit=8):
    vmem = pl.BlockSpec(memory_space=pltpu.VMEM)
    smem = pl.BlockSpec(memory_space=pltpu.SMEM)
    return pl.pallas_call(
        kernel,
        out_shape=shapes,
        in_specs=[smem] * scalars + [vmem] * n_in,
        out_specs=[vmem] * len(shapes),
        compiler_params=pltpu.CompilerParams(vmem_limit_bytes=limit * 1024 * 1024),
    )


def body(grid, context, target, weight, stale, trigger, aggregate, moment, second):
    rows = context.shape[0]
    width = context.shape[1]
    owned = weight.shape[0]
    blocks = trigger.shape[1]
    outer, inner, cores, n_sub = grid.sizes
    near, along, pair = grid.near(), grid.along(), grid.cores()
    f32, bf16 = jnp.float32, jnp.bfloat16
    shape = jax.ShapeDtypeStruct

    def move(value, shift):
        return lax.ppermute(value, AXES, grid.perm(shift))

    low = weight.astype(bf16)
    line = jnp.concatenate([move(low, d) for d in along[1:]], axis=0)
    mine = []
    for d in near:
        mine += [move(low, d), move(line, d)] if any(d) else [low, line]
    pieces = mine + [move(p, pair[1]) for p in mine]

    over_tokens = (((0,), (0,)), ((), ()))
    square = lax.dot_general(context, context, over_tokens, preferred_element_type=f32)
    high = lax.reduce_precision(square, 8, 7)
    g_high = high.astype(bf16)
    g_low = (square - high).astype(bf16)
    cross = lax.dot_general(context, target, over_tokens, preferred_element_type=f32)

    fits = blocks == outer * inner * cores and owned % (2 * EXTRA) == 0
    main = main_kernels if fits else main_plain
    stale_new, send, own, norms = main(
        grid, owned, blocks, rows, trigger[0], pieces, g_high, g_low, cross, stale[0]
    )
    got = move(send, pair[1])
    norms = norms + move(norms, pair[1])
    size = width // cores // len(near)
    keep, rest, *sends = call(
        functools.partial(near_kernel, len(near), owned),
        [shape((size, width), f32), shape(((len(near) - 1) * owned, width), bf16)]
        + [shape((size - owned, width), bf16)] * (len(near) - 1),
        2,
    )(own, got)
    got = [move(s, d) for s, d in zip(sends, near[1:])]
    far = [move(norms, d) for d in along[1:]]
    own, norms, *sends = call(
        functools.partial(along_kernel, outer, len(near)),
        [shape((owned, width), f32), shape(norms.shape, f32)]
        + [shape((owned, width), bf16)] * (outer - 1)
        + [shape((owned + EXTRA, width), bf16)] * (len(near) - 1),
        3 + len(far) + len(got),
    )(keep, rest, norms, *far, *got)
    got = [move(s, d) for s, d in zip(sends, along[1:] + near[1:])]
    aggregate_new, weight_new, moment_new, second_new, norms = call(
        functools.partial(final_kernel, outer, len(near)),
        [shape((owned, width), f32)] * 4 + [shape(norms.shape, f32)],
        2 + len(got) + 4,
    )(own, norms, *got, aggregate, weight, moment, second)
    return (aggregate_new, weight_new, moment_new, second_new, stale_new[None], norms[0, :blocks])


def solution(mesh):
    grid = Grid(mesh.shape["dp"], mesh.shape["sub"])
    split = P(("dp", "sub"), None)
    deep = P(("dp", "sub"), None, None)
    return jax.shard_map(
        functools.partial(body, grid),
        mesh=mesh,
        in_specs=(split, split, split, deep, split, split, split, split),
        out_specs=(split, split, split, split, deep, P()),
        check_vma=False,
    )
```
